32 devices in a mesh: gx: 4 (over y, x), gy: 4 (over z), gz: 2 (over core).
Axes of the slice: x: 2, y: 2, z: 4, core: 2. Of those that a mesh axis runs over, the one named last changes fastest.
Arguments:
- snapshots: bfloat16 [64, 3, 32, 16, 512], P(None, None, 'gy', 'gz', 'gx'), may hold values from -6 to 6
- modes: bfloat16 [128, 3, 32, 16, 512], P(None, None, 'gy', 'gz', 'gx'), may hold values from -0.0068359375 to 0.0068359375
Outputs:
- reduced_snapshots: float32 [128, 64], replicated
- reduced_features: float32 [128, 64], replicated
- gram_snap: float32 [128, 128], replicated
- gram_feature: float32 [128, 128], replicated
- gram_quad: float32 [64, 64], replicated
The draws below stay inside these ranges and needn't reach their ends.
All inputs are finite; a program needn't handle non-finite values.
Results may differ from the reference program's by a relative error of at most 0.0029.
Values may be sent and summed in bfloat16 or wider, within the bound.
A program may use at most 128 MiB of HBM per device.

```python
import jax
import jax.numpy as jnp
from jax import lax

MODES = 128
SNAPS = 64
NX = 512
NY = 32
NZ = 16


def levels(rng, shape, cuts, smallest, largest):
    def one(position, shards_of):
        heights = jax.random.uniform(jax.random.fold_in(jax.random.fold_in(rng, 6), position), (shards_of,), jnp.float32, smallest / len(cuts), largest / len(cuts))
        return jnp.repeat(jnp.exp(heights), shape[position] // shards_of).reshape((-1,) + (1,) * (len(shape) - position - 1))

    factor_of = one(*cuts[0])
    for cut in cuts[1:]:
        factor_of = factor_of * one(*cut)
    return factor_of


def bell_draw(stream_key, dims, scale, limit, shards=(), kind=jnp.bfloat16):
    array = scale * jax.random.normal(stream_key, dims, jnp.float32)
    if shards:
        array = array * levels(stream_key, dims, shards, -0.22, 0.18)
    return jnp.clip(array, -limit, limit).astype(kind)


def setup_inputs(seed: int = 0) -> dict:
    seeds = jax.random.split(jax.random.key(seed), 3)
    snapshots = bell_draw(seeds[0], (SNAPS, 3, NY, NZ, NX), 1.0, 6.0, ((2, 4), (3, 2), (4, 4)))
    modes = bell_draw(seeds[1], (MODES, 3, NY, NZ, NX), (3 * NX * NY * NZ) ** -0.5, 0.0068359375, ((2, 4), (3, 2), (4, 4)))
    return dict(snapshots=snapshots, modes=modes)


viscosity = 0.1


def stencil_terms(padded, direction, extent):
    pieces = [lax.slice_in_dim(padded, offset, offset + extent, axis=direction).astype(jnp.float32) for offset in range(5)]
    gradient = (8.0 * (pieces[3] - pieces[1]) - (pieces[4] - pieces[0])) / 12.0
    curvature = (16.0 * (pieces[3] + pieces[1]) - (pieces[4] + pieces[0]) - 30.0 * pieces[2]) / 12.0
    return gradient, curvature


def feature_field(velocity, padded_list):
    advect = jnp.zeros(velocity.shape, jnp.float32)
    laplace = jnp.zeros(velocity.shape, jnp.float32)
    for padded, direction, component in padded_list:
        gradient, curvature = stencil_terms(padded, direction, velocity.shape[direction])
        advect = advect + velocity[:, component:component + 1] * gradient
        laplace = laplace + curvature
    return (viscosity * laplace - advect).astype(jnp.bfloat16)


def one_snapshot(single):
    block = single[None]
    padded_wall = jnp.pad(block, ((0, 0), (0, 0), (2, 2), (0, 0), (0, 0)))
    padded_span = jnp.pad(block, ((0, 0), (0, 0), (0, 0), (2, 2), (0, 0)), mode="wrap")
    padded_stream = jnp.pad(block, ((0, 0), (0, 0), (0, 0), (0, 0), (2, 2)), mode="wrap")
    listed = ((padded_stream, 4, 0), (padded_wall, 2, 1), (padded_span, 3, 2))
    return feature_field(block.astype(jnp.float32), listed)[0]


def project(modes_flat, data_flat):
    return lax.dot_general(modes_flat, data_flat, (((1,), (1,)), ((), ())), preferred_element_type=jnp.float32)


def reference(snapshots, modes):
    features = lax.map(one_snapshot, snapshots)
    modes_flat = modes.reshape(modes.shape[0], -1)
    reduced_snapshots = project(modes_flat, snapshots.reshape(snapshots.shape[0], -1))
    reduced_features = project(modes_flat, features.reshape(features.shape[0], -1))
    high = lax.Precision.HIGHEST
    gram_snap = jnp.dot(reduced_snapshots, reduced_snapshots.T, precision=high, preferred_element_type=jnp.float32) / SNAPS
    gram_feature = jnp.dot(reduced_features, reduced_snapshots.T, precision=high, preferred_element_type=jnp.float32) / SNAPS
    products = jnp.dot(reduced_snapshots.T, reduced_snapshots, precision=high, preferred_element_type=jnp.float32) / MODES
    gram_quad = products * products
    return reduced_snapshots, reduced_features, gram_snap, gram_feature, gram_quad
```

```python
import functools

import jax
import jax.numpy as jnp
from jax import lax
from jax.experimental import pallas as pl
from jax.experimental.pallas import tpu as pltpu
from jax.sharding import PartitionSpec as P

viscosity = 0.1


def padded_2(cells, sides, width, closed):
    for axis, dim in sides:
        count = lax.axis_size(axis)
        ends = count if closed else count - 1
        head = lax.slice_in_dim(cells, 0, width, axis=dim)
        tail = lax.slice_in_dim(cells, cells.shape[dim] - width, cells.shape[dim], axis=dim)
        cells = jnp.concatenate(
            [
                lax.ppermute(tail, axis, [(i, (i + 1) % count) for i in range(ends)]),
                cells,
                lax.ppermute(head, axis, [((i + 1) % count, i) for i in range(ends)]),
            ],
            axis=dim,
        )
    return cells


def stencil_terms(padded, direction, extent):
    pieces = [
        lax.slice_in_dim(padded, offset, offset + extent, axis=direction).astype(jnp.float32)
        for offset in range(5)
    ]
    gradient = (8.0 * (pieces[3] - pieces[1]) - (pieces[4] - pieces[0])) / 12.0
    curvature = (16.0 * (pieces[3] + pieces[1]) - (pieces[4] + pieces[0]) - 30.0 * pieces[2]) / 12.0
    return (gradient, curvature)


def feature_field(velocity, padded_list):
    advect = jnp.zeros(velocity.shape, jnp.float32)
    laplace = jnp.zeros(velocity.shape, jnp.float32)
    for padded, direction, component in padded_list:
        gradient, curvature = stencil_terms(padded, direction, velocity.shape[direction])
        advect = advect + velocity[:, component : component + 1] * gradient
        laplace = laplace + curvature
    return (viscosity * laplace - advect).astype(jnp.bfloat16)


def project(modes_flat, data_flat):
    return lax.dot_general(
        modes_flat, data_flat, (((1,), (1,)), ((), ())), preferred_element_type=jnp.float32
    )


def local_features(snapshots):
    padded_stream = padded_2(snapshots, (("gx", 4),), 2, True)
    padded_span = padded_2(snapshots, (("gz", 3),), 2, True)
    padded_wall = padded_2(snapshots, (("gy", 2),), 2, False)
    velocity = snapshots.astype(jnp.float32)
    listed = ((padded_stream, 4, 0), (padded_wall, 2, 1), (padded_span, 3, 2))
    return feature_field(velocity, listed)


def gram_kernel(
    names, counts, snap_count, share_ref, snap_ref, feat_ref, gs_ref, gf_ref, gq_ref,
    total, slots, send_sem, recv_sem,
):
    bases = [sum(counts[:i]) for i in range(len(counts))]
    places = [lax.axis_index(name) for name in names]
    barrier = pltpu.get_barrier_semaphore()
    for name, count, place in zip(names, counts, places):
        for step in range(1, count):
            peer = lax.rem(place + step, count)
            pl.semaphore_signal(
                barrier, inc=1, device_id={name: peer}, device_id_type=pl.DeviceIdType.MESH
            )
    pl.semaphore_wait(barrier, sum(counts) - len(counts))

    for stage, (name, count, base, place) in enumerate(zip(names, counts, bases, places)):
        source = share_ref if stage == 0 else total.at[stage - 1]
        copies = []
        for step in range(1, count):
            peer = lax.rem(place + step, count)
            copy = pltpu.make_async_remote_copy(
                src_ref=source,
                dst_ref=slots.at[base + place],
                send_sem=send_sem.at[base + step],
                recv_sem=recv_sem.at[base + step],
                device_id={name: peer},
                device_id_type=pl.DeviceIdType.MESH,
            )
            copy.start()
            copies.append(copy)
        slots[base + place] = source[...]
        for copy in copies:
            copy.wait()
        added = slots[base]
        for index in range(1, count):
            added = added + slots[base + index]
        total[stage] = added

    combined = total[len(names) - 1]
    snap = combined[:, :snap_count]
    feat = combined[:, snap_count:]
    snap_ref[...] = snap
    feat_ref[...] = feat
    dot = functools.partial(
        lax.dot_general, precision=lax.Precision.HIGHEST, preferred_element_type=jnp.float32
    )
    gs_ref[...] = dot(snap, snap, (((1,), (1,)), ((), ()))) / snap_count
    gf_ref[...] = dot(feat, snap, (((1,), (1,)), ((), ()))) / snap_count
    turned = combined.T[:snap_count]
    products = dot(turned, turned, (((1,), (1,)), ((), ()))) / combined.shape[0]
    gq_ref[...] = products * products


def reduce_and_gram(share, snap_count):
    names = ("gz", "gy", "gx")
    counts = tuple(lax.axis_size(name) for name in names)
    mode_count, width = share.shape
    f32 = jnp.float32
    slot_count = sum(counts)
    vmem = pl.BlockSpec(memory_space=pltpu.VMEM)
    return tuple(pl.pallas_call(
        functools.partial(gram_kernel, names, counts, snap_count),
        out_shape=(
            jax.ShapeDtypeStruct((mode_count, snap_count), f32),
            jax.ShapeDtypeStruct((mode_count, width - snap_count), f32),
            jax.ShapeDtypeStruct((mode_count, mode_count), f32),
            jax.ShapeDtypeStruct((mode_count, mode_count), f32),
            jax.ShapeDtypeStruct((snap_count, snap_count), f32),
        ),
        in_specs=[vmem],
        out_specs=(vmem,) * 5,
        scratch_shapes=[
            pltpu.VMEM((len(names), mode_count, width), f32),
            pltpu.VMEM((slot_count, mode_count, width), f32),
            pltpu.SemaphoreType.DMA((slot_count,)),
            pltpu.SemaphoreType.DMA((slot_count,)),
        ],
        compiler_params=pltpu.CompilerParams(collective_id=0, has_side_effects=True),
        name="reduce_gram",
    )(share))


def shards(snapshots, modes):
    snap_count = snapshots.shape[0]
    mode_count = modes.shape[0]
    modes_flat = modes.reshape(mode_count, -1)
    snap_flat = snapshots.reshape(snap_count, -1)
    features = local_features(snapshots)
    feature_flat = features.reshape(snap_count, -1)
    stacked = jnp.concatenate([snap_flat, feature_flat], axis=0)
    return reduce_and_gram(project(modes_flat, stacked), snap_count)


def solution(mesh):
    return jax.shard_map(
        shards,
        mesh=mesh,
        in_specs=(P(None, None, "gy", "gz", "gx"), P(None, None, "gy", "gz", "gx")),
        out_specs=(P(), P(), P(), P(), P()),
        check_vma=False,
    )
```
